32 devices in a mesh: ctx: 8 (over y, x, core), qry: 4 (over z).
Axes of the slice: x: 2, y: 2, z: 4, core: 2. Of those that a mesh axis runs over, the one named last changes fastest.
Arguments:
- idx_query: bfloat16 [32, 8192], P('ctx', 'qry'), may hold values from -200 to 200
- idx_weight: bfloat16 [32, 64], P('ctx', 'qry'), may hold values from -3 to 3
- idx_keys: bfloat16 [16384, 128], P('ctx'), may hold values from -6 to 6
- q_latent: bfloat16 [32, 73728], P(('ctx', 'qry')), may hold values from -400 to 400
- latent_cache: bfloat16 [16384, 576], P('ctx'), may hold values from -20 to 20
- page_ids: int32 [32, 32], P(('ctx', 'qry')), may hold values from 0 to 255, as said below
Outputs:
- index_logp: float32 [32, 16384], P(('ctx', 'qry'))
- latent_out: bfloat16 [32, 65536], P(('ctx', 'qry'))
The draws below stay inside these ranges and needn't reach their ends.
Inputs may be any that keep to these rules, and one draw needn't show every extreme that they name: `page_ids`: each row names 32 distinct pages, and no page id appears twice in the 1 row of one device (aligned blocks of 1 row). Page p holds tokens p * 64 to p * 64 + 63; ctx index j holds pages j * 32 to (j + 1) * 32 - 1. Of the 32 ids in the rows of one device, at most 8 lie on one ctx index, and in every such block some ctx index holds exactly 8.
All inputs are finite; a program needn't handle non-finite values.
Results may differ from the reference program's by a relative error of at most 0.013.
Values may be sent and summed in bfloat16 or wider, within the bound.
A program may use at most 64 MiB of HBM per device.

```python
import math
import jax
import jax.numpy as jnp
from jax import lax

H_IDX = 64
D_IDX = 128
H = 128
D_LAT = 512
D_ROPE = 64
QK_NOPE = 128
DK = 576
PAGE = 64
TOPP = 32
CTX_DEV = 2048
QR_DEV = 1
MOST = 8
PAGES_DEV = 32
PAGES = 256
CTX = 16384
QROWS = 32


def draw_idx_query(key, part):
    norm_key = jax.random.fold_in(jax.random.fold_in(key, 11), 0)
    values = jnp.clip(jax.random.normal(norm_key, (QROWS, H_IDX * D_IDX), jnp.float32), -6.0, 6.0)
    return jnp.clip(values, -200.0, 200.0).astype(jnp.bfloat16)


def draw_idx_keys(key, part):
    norm_key = jax.random.fold_in(jax.random.fold_in(key, 13), 0)
    values = jnp.clip(jax.random.normal(norm_key, (CTX, D_IDX), jnp.float32), -6.0, 6.0) / math.sqrt(D_IDX)
    return jnp.clip(values, -6.0, 6.0).astype(jnp.bfloat16)


def draw_q_latent(key, part):
    norm_key = jax.random.fold_in(jax.random.fold_in(key, 17), 0)
    values = jnp.clip(jax.random.normal(norm_key, (QROWS, H, DK), jnp.float32), -6.0, 6.0)
    return jnp.clip(values, -400.0, 400.0).reshape(QROWS, H * DK).astype(jnp.bfloat16)


def draw_latent_cache(key, part):
    norm_key = jax.random.fold_in(jax.random.fold_in(key, 19), 0)
    values = jnp.clip(jax.random.normal(norm_key, (CTX, DK), jnp.float32), -6.0, 6.0)
    return jnp.clip(values, -20.0, 20.0).astype(jnp.bfloat16)


def draw_page_ids(key, part):
    shard_count = PAGES // PAGES_DEV
    wanted = QR_DEV * TOPP
    couple_count = shard_count * MOST
    heat_key, block_key = jax.random.split(jax.random.fold_in(key, 23))
    partition_load = jax.random.randint(heat_key, (shard_count,), 0, 4)
    couple_holder = jnp.arange(couple_count, dtype=jnp.int32) // MOST
    pair_copy = jnp.arange(couple_count, dtype=jnp.int32) % MOST

    def one_block(block_seed):
        seeds = jax.random.split(block_seed, 4)
        random_noise = jax.random.randint(seeds[0], (couple_count,), 0, 65536)
        compelled_pick = jax.random.randint(seeds[1], (), 0, shard_count)
        compelled_reward = jnp.where(couple_holder == compelled_pick, 1048576, 0)
        couple_score = (random_noise + partition_load[couple_holder] * 32768 + compelled_reward) * couple_count + jnp.arange(couple_count, dtype=jnp.int32)
        picked = lax.top_k(couple_score, wanted)[1]
        offset = jax.random.randint(seeds[2], (shard_count,), 0, PAGES_DEV)
        owner_shard = couple_holder[picked]
        local_page = (offset[owner_shard] + pair_copy[picked]) % PAGES_DEV
        page_list = owner_shard * PAGES_DEV + local_page
        shuffled = jax.random.permutation(seeds[3], page_list)
        return shuffled.reshape(QR_DEV, TOPP)
    block_seeds = jax.random.split(block_key, QROWS // QR_DEV)
    return jax.vmap(one_block)(block_seeds).reshape(QROWS, TOPP).astype(jnp.int32)


def block_scale(rng, dims, cuts, low, high):
    level, own = 1.0, jax.random.fold_in(rng, 6)
    for position, blocks in cuts:
        heights = jnp.exp(jax.random.uniform(jax.random.fold_in(own, position), (blocks,), jnp.float32, low / len(cuts), high / len(cuts)))
        level = level * jnp.repeat(heights, dims[position] // blocks).reshape([-1 if axis == position else 1 for axis in range(len(dims))])
    return level


def normal_values(key, dims, scale, most, cuts=(), kind=jnp.bfloat16):
    gain = block_scale(key, dims, cuts, -0.22, 0.18) if cuts else 1.0
    values = jax.random.normal(key, dims, jnp.float32) * scale * gain
    return jnp.minimum(jnp.maximum(values, -most), most).astype(kind)


def setup_inputs(seed: int = 0) -> dict:
    key_of = jax.random.split(jax.random.key(seed), 7)
    idx_query = draw_idx_query(jax.random.fold_in(key_of[6], 71), 0)
    idx_weight = normal_values(key_of[1], (QROWS, H_IDX), 0.7, 3.0, ((0, 8), (1, 4)))
    idx_keys = draw_idx_keys(jax.random.fold_in(key_of[6], 71), 0)
    q_latent = draw_q_latent(jax.random.fold_in(key_of[6], 71), 0)
    latent_cache = draw_latent_cache(jax.random.fold_in(key_of[6], 71), 0)
    page_ids = draw_page_ids(jax.random.fold_in(key_of[6], 71), 0)
    return dict(idx_query=idx_query, idx_weight=idx_weight, idx_keys=idx_keys, q_latent=q_latent, latent_cache=latent_cache, page_ids=page_ids)


def reference(idx_query, idx_weight, idx_keys, q_latent, latent_cache, page_ids):
    block_width = min(512, CTX_DEV)
    query_flat = idx_query.astype(jnp.float32).reshape(QROWS * H_IDX, D_IDX)
    head_weights = idx_weight.astype(jnp.float32)
    key_blocks = idx_keys.astype(jnp.float32).reshape(CTX // block_width, block_width, D_IDX)

    def index_block(key_block):
        head_dots = jnp.dot(query_flat, key_block.T)
        active = jnp.maximum(head_dots, 0.0).reshape(QROWS, H_IDX, block_width)
        return jnp.sum(active * head_weights[:, :, None], axis=1)

    blocks = lax.map(index_block, key_blocks)
    scores = jnp.moveaxis(blocks, 0, 1).reshape(QROWS, CTX)
    row_max = jnp.max(scores, axis=1, keepdims=True)
    row_total = jnp.sum(jnp.exp(scores - row_max), axis=1, keepdims=True)
    index_logp = scores - (row_max + jnp.log(row_total)) + jnp.log(CTX * 1.0)

    page_store = latent_cache.reshape(PAGES, PAGE, DK)
    logit_scale = (QK_NOPE + D_ROPE) ** -0.5

    def attend(pair):
        query_row, row_pages = pair
        key_rows = page_store[row_pages].reshape(TOPP * PAGE, DK)
        logits = jnp.dot(query_row.reshape(H, DK).astype(jnp.float32), key_rows.astype(jnp.float32).T) * logit_scale
        logit_max = jnp.max(logits, axis=1, keepdims=True)
        expo = jnp.exp(logits - logit_max)
        att_weights = (expo / jnp.sum(expo, axis=1, keepdims=True)).astype(jnp.bfloat16)
        mixed_rows = jnp.dot(att_weights, key_rows[:, :D_LAT], preferred_element_type=jnp.float32)
        return mixed_rows.astype(jnp.bfloat16).reshape(H * D_LAT)

    latent_out = lax.map(attend, (q_latent, page_ids))
    return index_logp, latent_out
```

```python
import functools

import jax
import jax.numpy as jnp
from jax import lax
from jax.experimental import pallas as pl
from jax.experimental.pallas import tpu as pltpu
from jax.sharding import PartitionSpec as P

H_IDX = 64
D_IDX = 128
H = 128
D_LAT = 512
D_ROPE = 64
QK_NOPE = 128
PAGE = 64

MESH = pl.DeviceIdType.MESH
LOG2E = 1.4426950408889634
NEG = -1e30
LANES = 128
PARTS = 8


def flip(a, r, n):
    out, bit = 0, 1
    while bit < n:
        x, y = (a // bit) % 2, (r // bit) % 2
        out = out + bit * (x + y - 2 * x * y)
        bit *= 2
    return out


def repeat(lo, hi, body):
    if hi - lo <= 8:
        for i in range(lo, hi):
            body(i)
    else:

        def step(i, carry):
            body(i)
            return carry

        lax.fori_loop(lo, hi, step, 0)


def kernel(
    n, g,
    heads_ref, gains_ref, cache_ref, keys_ref, latent_ref, pages_ref,
    logp_ref, out_ref,
    head_rows, mine_ref, pairs, q_send, q_in, queries, flat_query, wide_gains,
    zed, idx, keys_all, raw, kt, tab_send, tab_in, tabs,
    osend, orecv, tsend, trecv, ssend, srecv,
    up_sem, z_s, z_r, i_s, i_r, k_s, k_r, q_s, q_r, p_s, p_r, o_s, o_r, t_s, t_r, s_s, s_r, e_s, e_r,
    loc, tab_sem,
):
    c = lax.axis_index("ctx")
    z = lax.axis_index("qry")
    core, chip = c % 2, c // 2
    chips = n // 2
    ctx_dev = keys_ref.shape[0]
    width = cache_ref.shape[0]
    half = H // 2
    hb = mine_ref.shape[2]
    topp = pages_ref.shape[1]
    pages_dev = ctx_dev // PAGE
    most = max(1, 2 * topp // n)
    part = ctx_dev // PARTS

    barrier = pltpu.get_barrier_semaphore()

    def mate(m):
        return (2 * flip(chip, m, chips) + core, z)

    partner = (flip(c, 1, n), z)

    def greet(device):
        pl.semaphore_signal(barrier, inc=1, device_id=device, device_id_type=MESH)

    repeat(1, chips, lambda m: greet(mate(m)))
    greet(partner)
    for u in range(1, g):

        @pl.when(u > z)
        def _():
            greet((c, u))

    own_k = pltpu.make_async_copy(cache_ref, raw.at[0], loc.at[1])
    own_k.start()
    own_e = pltpu.make_async_copy(keys_ref, keys_all.at[core], loc.at[5])
    own_e.start()

    for p in range(half):
        pairs[p : p + 1, :] = latent_ref[:, p * 2 * width : (p + 1) * 2 * width].astype(
            jnp.float32
        )
    q_send[...] = pairs[...].astype(jnp.bfloat16)

    across = lax.broadcasted_iota(jnp.int32, (topp, topp), 1)
    down = lax.broadcasted_iota(jnp.int32, (topp, topp), 0)
    row_ids = jnp.broadcast_to(pages_ref[...], (topp, topp))
    col_ids = jnp.sum(jnp.where(across == down, row_ids, 0), axis=1, keepdims=True)
    bits = pages_dev.bit_length() - 1
    row_home, col_home = row_ids >> bits, col_ids >> bits
    rank = jnp.sum(
        jnp.where((row_home == col_home) & (across < down), 1, 0), axis=1, keepdims=True
    )
    lane = lax.broadcasted_iota(jnp.int32, (topp, LANES), 1)
    slot = jnp.where(lane < most, lane, lane - most)
    turn = jnp.where(lane < most, core, 1 - core)
    page = col_ids - (col_home << bits) + 1
    for m in range(chips):
        home = 2 * flip(chip, m, chips) + turn
        hit = (col_home == home) & (rank == slot) & (lane < 2 * most)
        tab_send[m] = jnp.sum(jnp.where(hit, page, 0), axis=0, keepdims=True) - 1

    own_tab = pltpu.make_async_copy(tab_send.at[0], tabs.at[0], tab_sem.at[0])

    for h in range(hb):
        piece = heads_ref[:, h * D_IDX : (h + 1) * D_IDX].astype(jnp.float32)
        for r in range(g):
            head_rows[r, h : h + 1, :] = piece[r : r + 1]
    eye = lax.broadcasted_iota(jnp.int32, (hb, hb), 0) == lax.broadcasted_iota(
        jnp.int32, (hb, hb), 1
    )
    gains = gains_ref[...].astype(jnp.float32)
    for r in range(g):
        mine_ref[r, 0] = head_rows[r].astype(jnp.bfloat16)
        gain = jnp.sum(jnp.where(eye, gains[r : r + 1], 0.0), axis=1, keepdims=True)
        mine_ref[r, 1] = jnp.broadcast_to(gain, (hb, D_IDX)).astype(jnp.bfloat16)

    def remote(src, dst, send, recv, device):
        return pltpu.make_async_remote_copy(
            src_ref=src, dst_ref=dst, send_sem=send, recv_sem=recv,
            device_id=device, device_id_type=MESH,
        )

    def z_copy(r):
        peer = flip(z, r, g)
        return remote(mine_ref.at[peer], zed.at[z], z_s.at[r], z_r.at[r], (c, peer))

    def k_copy(t):
        at = pl.ds(t * part, part)
        return remote(cache_ref.at[:, at], raw.at[1, :, at], k_s.at[t], k_r.at[t], partner)

    def e_copy():
        return remote(keys_ref, keys_all.at[core], e_s, e_r, partner)

    def q_copy(m):
        return remote(q_send, q_in.at[m], q_s.at[m], q_r.at[m], mate(m))

    def p_copy(m):
        return remote(tab_send.at[m], tab_in.at[m], p_s.at[m], p_r.at[m], mate(m))

    def i_copy(m):
        return remote(zed, idx.at[m], i_s.at[m], i_r.at[m], mate(m))

    def o_copy(m):
        return remote(osend.at[m], orecv.at[m], o_s.at[m], o_r.at[m], mate(m))

    def t_copy(m):
        return remote(tsend.at[m], trecv.at[m], t_s.at[m], t_r.at[m], mate(m))

    def s_copy(m):
        return remote(ssend.at[m], srecv.at[chip], s_s.at[m], s_r.at[m], mate(m))

    with jax.named_scope("w_barrier"):
        pl.semaphore_wait(barrier, chips + z)
    for u in range(g - 1):

        @pl.when(u < z)
        def _():
            pl.semaphore_signal(up_sem, inc=1, device_id=(c, u), device_id_type=MESH)

    repeat(1, chips, lambda m: p_copy(m).start())
    repeat(1, chips, lambda m: q_copy(chips - m).start())
    for t in range(PARTS):
        k_copy(t).start()
    e_copy().start()
    own_tab.start()
    own_z = pltpu.make_async_copy(mine_ref.at[z], zed.at[z], loc.at[0])
    own_z.start()
    for r in range(1, g):

        @pl.when(flip(z, r, g) < z)
        def _():
            z_copy(r).start()

    def turn_part(side, t):
        pages = part // PAGE
        kt[side, t * pages : (t + 1) * pages] = jnp.transpose(
            raw[side, :, t * part : (t + 1) * part]
        ).reshape(pages, PAGE, width)

    with jax.named_scope("xpose"):
        own_k.wait()
        for t in range(PARTS):
            turn_part(0, t)

    with jax.named_scope("w_up"):

        @pl.when(z < g - 1)
        def _():
            pl.semaphore_wait(up_sem, g - 1 - z)

    for r in range(1, g):

        @pl.when(flip(z, r, g) > z)
        def _():
            z_copy(r).start()

    def tab_copy(m):
        return pltpu.make_async_copy(tab_in.at[m], tabs.at[m], tab_sem.at[m])

    def take_tab(m):
        p_copy(m).wait_recv()
        tab_copy(m).start()

    with jax.named_scope("w_tab"):
        repeat(1, chips, take_tab)
        own_tab.wait()
        repeat(1, chips, lambda m: tab_copy(m).wait())

    with jax.named_scope("w_k"):
        for t in range(PARTS):
            k_copy(t).wait_recv()
            turn_part(1, t)

    with jax.named_scope("w_z"):
        own_z.wait()
        repeat(1, g, lambda r: z_copy(r).wait_recv())
        own_i = pltpu.make_async_copy(zed, idx.at[0], loc.at[3])
        own_i.start()
        repeat(1, chips, lambda m: i_copy(m).start())

    scale = ((QK_NOPE + D_ROPE) ** -0.5) * LOG2E
    low = lax.broadcasted_iota(jnp.int32, (1, LANES), 1) < PAGE
    slots = 2 * most

    def attend(m):
        query = q_send[...] if isinstance(m, int) and m == 0 else q_in[m]
        queries[:half, :] = query[:, :width]
        queries[half:, :] = query[:, width:]
        ids = [tabs[m, 0, s] for s in range(slots)]
        flags = [jnp.minimum(p, 0).astype(jnp.float32) * -NEG for p in ids]
        keys = jnp.concatenate(
            [kt[s // most, jnp.maximum(ids[s], 0)] for s in range(slots)], axis=0
        )
        bias = jnp.concatenate(
            [jnp.where(low, flags[s], flags[s + 1]) for s in range(0, slots, 2)], axis=1
        )
        dots = lax.dot_general(
            queries[...], keys, (((1,), (1,)), ((), ())), preferred_element_type=jnp.float32
        ) * scale + bias
        top = jnp.max(dots, axis=1, keepdims=True)
        expo = jnp.exp2(dots - top)
        mass = jnp.sum(expo, axis=1, keepdims=True)
        mixed = jnp.dot(
            expo.astype(jnp.bfloat16), keys[:, :D_LAT], preferred_element_type=jnp.float32
        ).astype(jnp.bfloat16)
        osend[m, :, :D_LAT] = mixed[:half]
        osend[m, :, D_LAT:] = mixed[half:]
        lane = lax.broadcasted_iota(jnp.int32, (H, LANES), 1)
        tsend[m] = jnp.transpose(jnp.where(lane == 0, top, mass))[:8]

    def serve(m):
        with jax.named_scope("w_q"):
            q_copy(m).wait_recv()
        with jax.named_scope("att"):
            attend(m)
        t_copy(m).start()
        o_copy(m).start()

    if chips <= 4:
        serve(chips - 1)
        with jax.named_scope("att0"):
            attend(0)
        for m in range(1, chips - 1):
            serve(m)
    else:
        attend(0)
        repeat(1, chips, lambda m: serve(chips - m))

    with jax.named_scope("w_idx"):
        own_i.wait()
        own_e.wait()
        e_copy().wait_recv()
        repeat(1, chips, lambda m: i_copy(m).wait_recv())
    count = g * hb
    block = min(256, ctx_dev)
    most_rows = min(4, chips)

    def lay(r):
        rows = idx[r]
        flat_query[r] = rows[:, 0].reshape(count, D_IDX)
        wide_gains[r] = rows[:, 1].reshape(count, D_IDX).astype(jnp.float32)

    def score(b):
        for s in range(2 * ctx_dev // block):
            at = (s * block) % ctx_dev
            keys = keys_all[s * block // ctx_dev, at : at + block, :]
            dots = lax.dot_general(
                flat_query[pl.ds(most_rows * b, most_rows)].reshape(most_rows * count, D_IDX),
                keys, (((1,), (1,)), ((), ())), preferred_element_type=jnp.float32,
            )
            for j in range(most_rows):
                gain = wide_gains[most_rows * b + j]
                sums = [
                    jnp.sum(
                        jnp.maximum(
                            dots[j * count : (j + 1) * count, t * LANES : (t + 1) * LANES], 0.0
                        ) * gain,
                        axis=0, keepdims=True,
                    )
                    for t in range(block // LANES)
                ]
                ssend[most_rows * b + j, :, s * block : (s + 1) * block] = jnp.concatenate(
                    sums, axis=1
                )

    with jax.named_scope("index"):
        repeat(0, chips, lay)
        if chips > most_rows:

            def step(b, carry):
                score(b)
                return carry

            lax.fori_loop(0, chips // most_rows, step, 0)
        else:
            score(0)
    repeat(1, chips, lambda m: s_copy(m).start())
    own_s = pltpu.make_async_copy(ssend.at[0], srecv.at[chip], loc.at[4])
    own_s.start()

    def arrive(m):
        t_copy(m).wait_recv()
        o_copy(m).wait_recv()

    with jax.named_scope("w_o"):
        repeat(1, chips, arrive)
    with jax.named_scope("mix"):
        columns = [jnp.transpose(tsend[0] if m == 0 else trecv[m]) for m in range(chips)]
        tops = [v[:, 0:1] for v in columns]
        best = functools.reduce(jnp.maximum, tops)
        weights = [jnp.exp2(t - best) for t in tops]
        mass = functools.reduce(jnp.add, [w * v[:, 1:2] for w, v in zip(weights, columns)])
        shares = [w / mass for w in weights]
        for h in range(2):
            at = slice(h * D_LAT, (h + 1) * D_LAT)
            mixed = jnp.zeros((half, D_LAT), jnp.float32)
            for m in range(chips):
                value = osend[0, :, at] if m == 0 else orecv[m, :, at]
                mixed = mixed + value.astype(jnp.float32) * shares[m][h * half : (h + 1) * half]
            out_ref[:, at] = mixed.astype(jnp.bfloat16)

    own_s.wait()

    def take_scores(m):
        remote(
            ssend.at[m], srecv.at[flip(chip, m, chips)], s_s.at[m], s_r.at[m], mate(m)
        ).wait_recv()

    with jax.named_scope("w_s"):
        repeat(1, chips, take_scores)
    with jax.named_scope("logp"):
        table = srecv[...]
        row_max = jnp.max(table)
        row_total = jnp.sum(jnp.exp(table - row_max), keepdims=True)
        logp_ref[...] = table - (row_max + jnp.log(row_total)) + jnp.log(
            jnp.full((1, 1, 1), n * ctx_dev, jnp.float32)
        )

    with jax.named_scope("fin"):
        repeat(1, g, lambda r: z_copy(r).wait_send())
        for t in range(PARTS):
            k_copy(t).wait_send()
        e_copy().wait_send()

        def sent(m):
            p_copy(m).wait_send()
            q_copy(m).wait_send()
            o_copy(m).wait_send()
            t_copy(m).wait_send()
            i_copy(m).wait_send()
            s_copy(m).wait_send()

        repeat(1, chips, sent)


def per_device(n, g, idx_query, idx_weight, idx_keys, q_latent, latent_cache, page_ids):
    hb = H_IDX // g
    ctx_dev, width = idx_keys.shape[0], latent_cache.shape[1]
    chips = n // 2
    half = H // 2
    dma = pltpu.SemaphoreType.DMA
    bf16, f32, i32 = jnp.bfloat16, jnp.float32, jnp.int32
    anywhere = pl.BlockSpec(memory_space=pl.ANY)
    vmem = pl.BlockSpec(memory_space=pltpu.VMEM)
    logp, out = pl.pallas_call(
        functools.partial(kernel, n, g),
        out_shape=(
            jax.ShapeDtypeStruct((chips, 1, 2 * ctx_dev), f32),
            jax.ShapeDtypeStruct((half, 2 * D_LAT), bf16),
        ),
        in_specs=[vmem, vmem, anywhere, anywhere, vmem, vmem],
        out_specs=(vmem, vmem),
        scratch_shapes=[
            pltpu.VMEM((g, hb, D_IDX), f32),
            pltpu.VMEM((g, 2, hb, D_IDX), bf16),
            pltpu.VMEM((half, 2 * width), f32),
            pltpu.VMEM((half, 2 * width), bf16),
            pltpu.VMEM((chips, half, 2 * width), bf16),
            pltpu.VMEM((H, width), bf16),
            pltpu.VMEM((chips, g * hb, D_IDX), bf16),
            pltpu.VMEM((chips, g * hb, D_IDX), f32),
            pltpu.VMEM((g, 2, hb, D_IDX), bf16),
            pltpu.VMEM((chips, g, 2, hb, D_IDX), bf16),
            pltpu.VMEM((2, ctx_dev, D_IDX), bf16),
            pltpu.VMEM((2, width, ctx_dev), bf16),
            pltpu.VMEM((2, ctx_dev // PAGE, PAGE, width), bf16),
            pltpu.VMEM((chips, 1, LANES), i32),
            pltpu.VMEM((chips, 1, LANES), i32),
            pltpu.SMEM((chips, 1, LANES), i32),
            pltpu.VMEM((chips, half, 2 * D_LAT), bf16),
            pltpu.VMEM((chips, half, 2 * D_LAT), bf16),
            pltpu.VMEM((chips, 8, LANES), f32),
            pltpu.VMEM((chips, 8, LANES), f32),
            pltpu.VMEM((chips, 1, 2 * ctx_dev), f32),
            pltpu.VMEM((chips, 1, 2 * ctx_dev), f32),
            pltpu.SemaphoreType.REGULAR,
            dma((g,)), dma((g,)),
            dma((chips,)), dma((chips,)),
            dma((PARTS,)), dma((PARTS,)),
            dma((chips,)), dma((chips,)),
            dma((chips,)), dma((chips,)),
            dma((chips,)), dma((chips,)),
            dma((chips,)), dma((chips,)),
            dma((chips,)), dma((chips,)),
            dma, dma,
            dma((6,)), dma((chips,)),
        ],
        compiler_params=pltpu.CompilerParams(
            collective_id=0, has_side_effects=True, vmem_limit_bytes=60 * 1024 * 1024
        ),
    )(idx_query, idx_weight, latent_cache.T, idx_keys, q_latent, page_ids)
    return logp.reshape(1, n * ctx_dev), out.reshape(1, H * D_LAT)


def solution(mesh):
    in_specs = (
        P("ctx", "qry"),
        P("ctx", "qry"),
        P("ctx", None),
        P(("ctx", "qry"), None),
        P("ctx", None),
        P(("ctx", "qry"), None),
    )
    out_specs = (P(("ctx", "qry"), None), P(("ctx", "qry"), None))
    return jax.shard_map(
        functools.partial(per_device, mesh.shape["ctx"], mesh.shape["qry"]),
        mesh=mesh, in_specs=in_specs, out_specs=out_specs, check_vma=False,
    )
```

```python
import functools

import jax
import jax.numpy as jnp
from jax import lax
from jax.experimental import pallas as pl
from jax.experimental.pallas import tpu as pltpu
from jax.sharding import PartitionSpec as P

H_IDX = 64
D_IDX = 128
H = 128
D_LAT = 512
D_ROPE = 64
QK_NOPE = 128
PAGE = 64

MESH = pl.DeviceIdType.MESH
LOG2E = 1.4426950408889634
NEG = -1e30
LANES = 128
PARTS = 8
VMEM_MIB = 60


def flip(a, r, n):
    out, bit = 0, 1
    while bit < n:
        x, y = (a // bit) % 2, (r // bit) % 2
        out = out + bit * (x + y - 2 * x * y)
        bit *= 2
    return out


def repeat(lo, hi, body):
    if hi - lo <= 8:
        for i in range(lo, hi):
            body(i)
    else:

        def step(i, carry):
            body(i)
            return carry

        lax.fori_loop(lo, hi, step, 0)


def kernel(
    n, g,
    heads_ref, gains_ref, cache_ref, keys_ref, latent_ref, pages_ref,
    logp_ref, out_ref,
    head_rows, mine_ref, pairs, q_send, q_in, queries, flat_query, wide_gains,
    zed, pack, idx, keys_all, raw, kt, tab_send, tab_in, tabs, lines,
    osend, orecv, tsend, trecv, ssend, srecv,
    up_sem, z_s, z_r, i_s, i_r, k_s, k_r, q_s, q_r, p_s, p_r, o_s, o_r, t_s, t_r, s_s, s_r, e_s, e_r,
    loc, tab_sem,
):
    c = lax.axis_index("ctx")
    z = lax.axis_index("qry")
    core, chip = c % 2, c // 2
    chips = n // 2
    ctx_dev = keys_ref.shape[0]
    width = cache_ref.shape[0]
    half = H // 2
    hb = mine_ref.shape[2]
    topp = pages_ref.shape[1]
    pages_dev = ctx_dev // PAGE
    most = max(1, 2 * topp // n)
    part = ctx_dev // PARTS
    relay = chips == 4

    barrier = pltpu.get_barrier_semaphore()

    def mate(m):
        return (2 * flip(chip, m, chips) + core, z)

    partner = (flip(c, 1, n), z)

    def greet(device):
        pl.semaphore_signal(barrier, inc=1, device_id=device, device_id_type=MESH)

    repeat(1, chips, lambda m: greet(mate(m)))
    greet(partner)
    for u in range(1, g):

        @pl.when(u > z)
        def _():
            greet((c, u))

    own_k = pltpu.make_async_copy(cache_ref, raw.at[0], loc.at[1])
    own_k.start()
    own_e = pltpu.make_async_copy(keys_ref, keys_all.at[core], loc.at[5])
    own_e.start()

    for p in range(half):
        pairs[p : p + 1, :] = latent_ref[:, p * 2 * width : (p + 1) * 2 * width].astype(
            jnp.float32
        )
    q_send[...] = pairs[...].astype(jnp.bfloat16)

    across = lax.broadcasted_iota(jnp.int32, (topp, topp), 1)
    down = lax.broadcasted_iota(jnp.int32, (topp, topp), 0)
    row_ids = jnp.broadcast_to(pages_ref[...], (topp, topp))
    col_ids = jnp.sum(jnp.where(across == down, row_ids, 0), axis=1, keepdims=True)
    bits = pages_dev.bit_length() - 1
    row_home, col_home = row_ids >> bits, col_ids >> bits
    rank = jnp.sum(
        jnp.where((row_home == col_home) & (across < down), 1, 0), axis=1, keepdims=True
    )
    lane = lax.broadcasted_iota(jnp.int32, (topp, LANES), 1)
    slot = jnp.where(lane < most, lane, lane - most)
    turn = jnp.where(lane < most, core, 1 - core)
    page = col_ids - (col_home << bits) + 1
    for m in range(chips):
        home = 2 * flip(chip, m, chips) + turn
        hit = (col_home == home) & (rank == slot) & (lane < 2 * most)
        tab_send[m] = jnp.sum(jnp.where(hit, page, 0), axis=0, keepdims=True) - 1

    for h in range(hb):
        piece = heads_ref[:, h * D_IDX : (h + 1) * D_IDX].astype(jnp.float32)
        for r in range(g):
            head_rows[r, h : h + 1, :] = piece[r : r + 1]
    eye = lax.broadcasted_iota(jnp.int32, (hb, hb), 0) == lax.broadcasted_iota(
        jnp.int32, (hb, hb), 1
    )
    gains = gains_ref[...].astype(jnp.float32)
    for r in range(g):
        mine_ref[r, 0] = head_rows[r].astype(jnp.bfloat16)
        gain = jnp.sum(jnp.where(eye, gains[r : r + 1], 0.0), axis=1, keepdims=True)
        mine_ref[r, 1] = jnp.broadcast_to(gain, (hb, D_IDX)).astype(jnp.bfloat16)

    def remote(src, dst, send, recv, device):
        return pltpu.make_async_remote_copy(
            src_ref=src, dst_ref=dst, send_sem=send, recv_sem=recv,
            device_id=device, device_id_type=MESH,
        )

    def z_copy(r):
        peer = flip(z, r, g)
        return remote(mine_ref.at[peer], zed.at[z], z_s.at[r], z_r.at[r], (c, peer))

    def k_copy(t):
        at = pl.ds(t * part, part)
        return remote(cache_ref.at[:, at], raw.at[1, :, at], k_s.at[t], k_r.at[t], partner)

    def e_copy():
        return remote(keys_ref, keys_all.at[core], e_s, e_r, partner)

    def q_copy(m):
        return remote(q_send, q_in.at[m], q_s.at[m], q_r.at[m], mate(m))

    def q_half(m, h):
        at = pl.ds(h * half // 2, half // 2)
        k = 2 * (m - 1) + h
        return remote(q_send.at[at], q_in.at[m, at], q_s.at[k], q_r.at[k], mate(m))

    def q_relay(h):
        at = pl.ds(h * half // 2, half // 2)
        k = 4 + h
        return remote(
            q_in.at[1 + h, at], q_in.at[3, at], q_s.at[k], q_r.at[k], mate(2 - h)
        )

    def q_wait(m):
        if not relay:
            q_copy(m).wait_recv()
        elif m == 3:
            q_relay(0).wait_recv()
            q_relay(1).wait_recv()
        else:
            q_half(m, 2 - m).wait_recv()

    def p_copy(m):
        return remote(tab_send.at[m], tab_in.at[m], p_s.at[m], p_r.at[m], mate(m))

    def i_copy(m):
        return remote(pack, idx.at[m], i_s.at[m], i_r.at[m], mate(m))

    def o_copy(m):
        return remote(osend.at[m], orecv.at[m], o_s.at[m], o_r.at[m], mate(m))

    def t_copy(m):
        return remote(tsend.at[m], trecv.at[m], t_s.at[m], t_r.at[m], mate(m))

    def s_copy(m):
        return remote(ssend.at[m], srecv.at[chip], s_s.at[m], s_r.at[m], mate(m))

    with jax.named_scope("w_barrier"):
        pl.semaphore_wait(barrier, chips + z)
    for u in range(g - 1):

        @pl.when(u < z)
        def _():
            pl.semaphore_signal(up_sem, inc=1, device_id=(c, u), device_id_type=MESH)

    repeat(1, chips, lambda m: p_copy(m).start())
    if relay:
        for h in range(2):
            for m in (1, 2):
                q_half(m, (m - 1 + h) % 2).start()
    else:
        repeat(1, chips, lambda m: q_copy(chips - m).start())
    for t in range(PARTS):
        k_copy(t).start()
    e_copy().start()

    own_tab = pltpu.make_async_copy(tab_send.at[0], tabs.at[0], tab_sem.at[0])
    own_tab.start()

    own_z = pltpu.make_async_copy(mine_ref.at[z], zed.at[z], loc.at[0])
    own_z.start()
    for r in range(1, g):

        @pl.when(flip(z, r, g) < z)
        def _():
            z_copy(r).start()

    def turn_part(side, t):
        pages = part // PAGE
        kt[side, t * pages : (t + 1) * pages] = jnp.transpose(
            raw[side, :, t * part : (t + 1) * part]
        ).reshape(pages, PAGE, width)

    with jax.named_scope("xpose"):
        own_k.wait()
        for t in range(PARTS):
            turn_part(0, t)

    with jax.named_scope("relay"):
        if relay:
            for h in range(2):
                q_half(1 + h, h).wait_recv()
                q_relay(h).start()

    def tab_copy(m):
        return pltpu.make_async_copy(tab_in.at[m], tabs.at[m], tab_sem.at[m])

    def take_tab(m):
        p_copy(m).wait_recv()
        tab_copy(m).start()

    with jax.named_scope("w_up"):

        @pl.when(z < g - 1)
        def _():
            pl.semaphore_wait(up_sem, g - 1 - z)

    for r in range(1, g):

        @pl.when(flip(z, r, g) > z)
        def _():
            z_copy(r).start()

    def take_keys(t):
        k_copy(t).wait_recv()
        turn_part(1, t)

    with jax.named_scope("w_k"):
        for t in range(PARTS - 2):
            take_keys(t)

    with jax.named_scope("w_z"):
        own_z.wait()
        repeat(1, g, lambda r: z_copy(r).wait_recv())
        spread = lax.broadcasted_iota(jnp.int32, (hb, D_IDX), 1)
        blend = jnp.zeros((hb, D_IDX), jnp.float32)
        for r in range(g):
            pack[r] = zed[r, 0]
            blend = jnp.where(spread == r, zed[r, 1].astype(jnp.float32), blend)
        pack[g] = blend.astype(jnp.bfloat16)
        own_i = pltpu.make_async_copy(pack, idx.at[0], loc.at[3])
        own_i.start()
        repeat(1, chips, lambda m: i_copy(m).start())

    with jax.named_scope("w_tab"):
        repeat(1, chips, take_tab)

    with jax.named_scope("w_k2"):
        for t in range(PARTS - 2, PARTS):
            take_keys(t)

    with jax.named_scope("w_tab2"):
        own_tab.wait()
        repeat(1, chips, lambda m: tab_copy(m).wait())

    scale = ((QK_NOPE + D_ROPE) ** -0.5) * LOG2E
    low = lax.broadcasted_iota(jnp.int32, (1, LANES), 1) < PAGE
    slots = 2 * most

    def attend(m):
        query = q_send[...] if isinstance(m, int) and m == 0 else q_in[m]
        queries[:half, :] = query[:, :width]
        queries[half:, :] = query[:, width:]
        ids = [tabs[m, 0, s] for s in range(slots)]
        flags = [jnp.minimum(p, 0).astype(jnp.float32) * -NEG for p in ids]
        keys = jnp.concatenate(
            [kt[s // most, jnp.maximum(ids[s], 0)] for s in range(slots)], axis=0
        )
        bias = jnp.concatenate(
            [jnp.where(low, flags[s], flags[s + 1]) for s in range(0, slots, 2)], axis=1
        )
        dots = lax.dot_general(
            queries[...], keys, (((1,), (1,)), ((), ())), preferred_element_type=jnp.float32
        ) * scale + bias
        top = jnp.max(dots, axis=1, keepdims=True)
        expo = jnp.exp2(dots - top)
        mass = jnp.sum(expo, axis=1, keepdims=True)
        mixed = jnp.dot(
            expo.astype(jnp.bfloat16), keys[:, :D_LAT], preferred_element_type=jnp.float32
        ).astype(jnp.bfloat16)
        osend[m, :, :D_LAT] = mixed[:half]
        osend[m, :, D_LAT:] = mixed[half:]
        lane = lax.broadcasted_iota(jnp.int32, (H, LANES), 1)
        tsend[m] = jnp.transpose(jnp.where(lane == 0, top, mass))[:8]

    def serve(m):
        with jax.named_scope("w_q"):
            q_wait(m)
        with jax.named_scope("att"):
            attend(m)
        t_copy(m).start()
        o_copy(m).start()

    count = g * hb
    block = min(256, ctx_dev)
    most_rows = min(4, chips)

    def lay(r):
        rows = idx[r]
        flat_query[r] = rows[:g].reshape(count, D_IDX)
        tile = rows[g].astype(jnp.float32)
        for u in range(g):
            wide_gains[r, u * hb : (u + 1) * hb] = jnp.broadcast_to(
                tile[:, u : u + 1], (hb, D_IDX)
            )

    def score(b):
        for s in range(2 * ctx_dev // block):
            at = (s * block) % ctx_dev
            keys = keys_all[s * block // ctx_dev, at : at + block, :]
            dots = lax.dot_general(
                flat_query[pl.ds(most_rows * b, most_rows)].reshape(most_rows * count, D_IDX),
                keys, (((1,), (1,)), ((), ())), preferred_element_type=jnp.float32,
            )
            for j in range(most_rows):
                gain = wide_gains[most_rows * b + j]
                for t in range(block // LANES):
                    total = jnp.sum(
                        jnp.maximum(
                            dots[j * count : (j + 1) * count, t * LANES : (t + 1) * LANES], 0.0
                        ) * gain,
                        axis=0, keepdims=True,
                    )
                    line = s * (block // LANES) + t
                    lines[most_rows * b + j, line : line + 1, :] = total

    def index_rows():
        with jax.named_scope("w_idx"):
            own_i.wait()
            own_e.wait()
            e_copy().wait_recv()
            repeat(1, chips, lambda m: i_copy(m).wait_recv())
        with jax.named_scope("index"):
            repeat(0, chips, lay)
            if chips > most_rows:

                def step(b, carry):
                    score(b)
                    return carry

                lax.fori_loop(0, chips // most_rows, step, 0)
            else:
                score(0)
            ssend[...] = lines[...].astype(jnp.bfloat16)
        repeat(1, chips, lambda m: s_copy(m).start())

    def own_rows():
        with jax.named_scope("att0"):
            attend(0)

    if chips <= 4:
        for m in range(1, chips):
            serve(m)
        index_rows()
        own_rows()
    else:
        repeat(1, chips, lambda m: serve(chips - m))
        index_rows()
        own_rows()
    own_s = pltpu.make_async_copy(ssend.at[0], srecv.at[chip], loc.at[4])
    own_s.start()

    def arrive(m):
        t_copy(m).wait_recv()
        o_copy(m).wait_recv()

    own_s.wait()

    def take_scores(m):
        remote(
            ssend.at[m], srecv.at[flip(chip, m, chips)], s_s.at[m], s_r.at[m], mate(m)
        ).wait_recv()

    with jax.named_scope("w_s"):
        repeat(1, chips, take_scores)
    with jax.named_scope("logp"):
        table = srecv[...].astype(jnp.float32)
        row_max = jnp.max(table)
        row_total = jnp.sum(jnp.exp(table - row_max), keepdims=True)
        logp_ref[...] = table - (row_max + jnp.log(row_total)) + jnp.log(
            jnp.full((1, 1, 1), n * ctx_dev, jnp.float32)
        )

    with jax.named_scope("w_o"):
        repeat(1, chips, arrive)
    with jax.named_scope("mix"):
        columns = [jnp.transpose(tsend[0] if m == 0 else trecv[m]) for m in range(chips)]
        tops = [v[:, 0:1] for v in columns]
        best = functools.reduce(jnp.maximum, tops)
        weights = [jnp.exp2(t - best) for t in tops]
        mass = functools.reduce(jnp.add, [w * v[:, 1:2] for w, v in zip(weights, columns)])
        shares = [w / mass for w in weights]
        for h in range(2):
            at = slice(h * D_LAT, (h + 1) * D_LAT)
            mixed = jnp.zeros((half, D_LAT), jnp.float32)
            for m in range(chips):
                value = osend[0, :, at] if m == 0 else orecv[m, :, at]
                mixed = mixed + value.astype(jnp.float32) * shares[m][h * half : (h + 1) * half]
            for p in range(half):
                start = (2 * p + h) * D_LAT
                out_ref[:, start : start + D_LAT] = mixed[p : p + 1].astype(jnp.bfloat16)

    with jax.named_scope("fin"):
        repeat(1, g, lambda r: z_copy(r).wait_send())
        for t in range(PARTS):
            k_copy(t).wait_send()
        e_copy().wait_send()

        def sent(m):
            p_copy(m).wait_send()
            if not relay:
                q_copy(m).wait_send()
            o_copy(m).wait_send()
            t_copy(m).wait_send()
            i_copy(m).wait_send()
            s_copy(m).wait_send()

        repeat(1, chips, sent)
        if relay:
            for h in range(2):
                q_half(1, h).wait_send()
                q_half(2, h).wait_send()
                q_relay(h).wait_send()


def per_device(n, g, idx_query, idx_weight, idx_keys, q_latent, latent_cache, page_ids):
    hb = H_IDX // g
    ctx_dev, width = idx_keys.shape[0], latent_cache.shape[1]
    chips = n // 2
    half = H // 2
    dma = pltpu.SemaphoreType.DMA
    bf16, f32, i32 = jnp.bfloat16, jnp.float32, jnp.int32
    hbm = pl.BlockSpec(memory_space=pltpu.HBM)
    vmem = pl.BlockSpec(memory_space=pltpu.VMEM)
    logp, out = pl.pallas_call(
        functools.partial(kernel, n, g),
        out_shape=(
            pltpu.VMEM((chips, 2 * ctx_dev // LANES, LANES), f32),
            pltpu.VMEM((1, H * D_LAT), bf16),
        ),
        in_specs=[vmem, vmem, hbm, hbm, vmem, vmem],
        out_specs=(vmem, vmem),
        scratch_shapes=[
            pltpu.VMEM((g, hb, D_IDX), f32),
            pltpu.VMEM((g, 2, hb, D_IDX), bf16),
            pltpu.VMEM((half, 2 * width), f32),
            pltpu.VMEM((half, 2 * width), bf16),
            pltpu.VMEM((chips, half, 2 * width), bf16),
            pltpu.VMEM((H, width), bf16),
            pltpu.VMEM((chips, g * hb, D_IDX), bf16),
            pltpu.VMEM((chips, g * hb, D_IDX), f32),
            pltpu.VMEM((g, 2, hb, D_IDX), bf16),
            pltpu.VMEM((g + 1, hb, D_IDX), bf16),
            pltpu.VMEM((chips, g + 1, hb, D_IDX), bf16),
            pltpu.VMEM((2, ctx_dev, D_IDX), bf16),
            pltpu.VMEM((2, width, ctx_dev), bf16),
            pltpu.VMEM((2, ctx_dev // PAGE, PAGE, width), bf16),
            pltpu.VMEM((chips, 1, LANES), i32),
            pltpu.VMEM((chips, 1, LANES), i32),
            pltpu.SMEM((chips, 1, LANES), i32),
            pltpu.VMEM((chips, 2 * ctx_dev // LANES, LANES), f32),
            pltpu.VMEM((chips, half, 2 * D_LAT), bf16),
            pltpu.VMEM((chips, half, 2 * D_LAT), bf16),
            pltpu.VMEM((chips, 8, LANES), f32),
            pltpu.VMEM((chips, 8, LANES), f32),
            pltpu.VMEM((chips, 2 * ctx_dev // LANES, LANES), bf16),
            pltpu.VMEM((chips, 2 * ctx_dev // LANES, LANES), bf16),
            pltpu.SemaphoreType.REGULAR,
            dma((g,)), dma((g,)),
            dma((chips,)), dma((chips,)),
            dma((PARTS,)), dma((PARTS,)),
            dma((max(6, chips),)), dma((max(6, chips),)),
            dma((chips,)), dma((chips,)),
            dma((chips,)), dma((chips,)),
            dma((chips,)), dma((chips,)),
            dma((chips,)), dma((chips,)),
            dma, dma,
            dma((6,)), dma((chips,)),
        ],
        compiler_params=pltpu.CompilerParams(
            collective_id=0, has_side_effects=True, vmem_limit_bytes=VMEM_MIB * 1024 * 1024
        ),
    )(idx_query, idx_weight, latent_cache.T, idx_keys, q_latent, page_ids)
    return logp.reshape(1, n * ctx_dev), out


def solution(mesh):
    in_specs = (
        P("ctx", "qry"),
        P("ctx", "qry"),
        P("ctx", None),
        P(("ctx", "qry"), None),
        P("ctx", None),
        P(("ctx", "qry"), None),
    )
    out_specs = (P(("ctx", "qry"), None), P(("ctx", "qry"), None))
    return jax.shard_map(
        functools.partial(per_device, mesh.shape["ctx"], mesh.shape["qry"]),
        mesh=mesh, in_specs=in_specs, out_specs=out_specs, check_vma=False,
    )
```

```python
import functools

import jax
import jax.numpy as jnp
from jax import lax
from jax.experimental import pallas as pl
from jax.experimental.pallas import tpu as pltpu
from jax.sharding import PartitionSpec as P

H_IDX = 64
D_IDX = 128
H = 128
D_LAT = 512
D_ROPE = 64
QK_NOPE = 128
PAGE = 64

MESH = pl.DeviceIdType.MESH
LOG2E = 1.4426950408889634
NEG = -1e30
LANES = 128
PARTS = 8
VMEM_MIB = 60


def flip(a, r, n):
    out, bit = 0, 1
    while bit < n:
        x, y = (a // bit) % 2, (r // bit) % 2
        out = out + bit * (x + y - 2 * x * y)
        bit *= 2
    return out


def repeat(lo, hi, body):
    if hi - lo <= 8:
        for i in range(lo, hi):
            body(i)
    else:

        def step(i, carry):
            body(i)
            return carry

        lax.fori_loop(lo, hi, step, 0)


def kernel(
    n, g,
    heads_in, gains_in, cache_ref, keys_ref, latent_in, pages_in,
    logp_ref, out_ref,
    heads_ref, gains_ref, latent_ref, pages_ref, head_rows, mine_ref, pairs, q_send, q_in, queries, flat_query, wide_gains,
    zed, pack, idx, keys_all, raw, kt, tab_send, tab_in, tabs, lines,
    osend, orecv, tsend, trecv, ssend, srecv,
    up_sem, z_s, z_r, i_s, i_r, k_s, k_r, q_s, q_r, p_s, p_r, o_s, o_r, t_s, t_r, s_s, s_r, e_s, e_r,
    loc, tab_sem,
):
    c = lax.axis_index("ctx")
    z = lax.axis_index("qry")
    core, chip = c % 2, c // 2
    chips = n // 2
    ctx_dev = keys_ref.shape[0]
    width = cache_ref.shape[0]
    half = H // 2
    hb = mine_ref.shape[2]
    topp = pages_ref.shape[1]
    pages_dev = ctx_dev // PAGE
    most = max(1, 2 * topp // n)
    part = ctx_dev // PARTS
    relay = chips == 4

    barrier = pltpu.get_barrier_semaphore()

    def mate(m):
        return (2 * flip(chip, m, chips) + core, z)

    partner = (flip(c, 1, n), z)

    def greet(device):
        pl.semaphore_signal(barrier, inc=1, device_id=device, device_id_type=MESH)

    repeat(1, chips, lambda m: greet(mate(m)))
    greet(partner)
    for u in range(1, g):

        @pl.when(u > z)
        def _():
            greet((c, u))

    early = [
        pltpu.make_async_copy(src, dst, loc.at[6 + i])
        for i, (src, dst) in enumerate((
            (latent_in, latent_ref), (pages_in, pages_ref),
            (heads_in, heads_ref), (gains_in, gains_ref),
        ))
    ]
    for copy in early:
        copy.start()
    own_k = pltpu.make_async_copy(cache_ref, raw.at[0], loc.at[1])
    own_k.start()
    own_e = pltpu.make_async_copy(keys_ref, keys_all.at[core], loc.at[5])
    own_e.start()

    early[0].wait()
    for p in range(half):
        pairs[p : p + 1, :] = latent_ref[:, p * 2 * width : (p + 1) * 2 * width].astype(
            jnp.float32
        )
    q_send[...] = pairs[...].astype(jnp.bfloat16)

    across = lax.broadcasted_iota(jnp.int32, (topp, topp), 1)
    down = lax.broadcasted_iota(jnp.int32, (topp, topp), 0)
    early[1].wait()
    row_ids = jnp.broadcast_to(pages_ref[...], (topp, topp))
    col_ids = jnp.sum(jnp.where(across == down, row_ids, 0), axis=1, keepdims=True)
    bits = pages_dev.bit_length() - 1
    row_home, col_home = row_ids >> bits, col_ids >> bits
    rank = jnp.sum(
        jnp.where((row_home == col_home) & (across < down), 1, 0), axis=1, keepdims=True
    )
    lane = lax.broadcasted_iota(jnp.int32, (topp, LANES), 1)
    slot = jnp.where(lane < most, lane, lane - most)
    turn = jnp.where(lane < most, core, 1 - core)
    page = col_ids - (col_home << bits) + 1
    for m in range(chips):
        home = 2 * flip(chip, m, chips) + turn
        hit = (col_home == home) & (rank == slot) & (lane < 2 * most)
        tab_send[m] = jnp.sum(jnp.where(hit, page, 0), axis=0, keepdims=True) - 1

    def remote(src, dst, send, recv, device):
        return pltpu.make_async_remote_copy(
            src_ref=src, dst_ref=dst, send_sem=send, recv_sem=recv,
            device_id=device, device_id_type=MESH,
        )

    def z_copy(r):
        peer = flip(z, r, g)
        return remote(mine_ref.at[peer], zed.at[z], z_s.at[r], z_r.at[r], (c, peer))

    def k_copy(t):
        at = pl.ds(t * part, part)
        return remote(cache_ref.at[:, at], raw.at[1, :, at], k_s.at[t], k_r.at[t], partner)

    def e_copy():
        return remote(keys_ref, keys_all.at[core], e_s, e_r, partner)

    def q_copy(m):
        return remote(q_send, q_in.at[m], q_s.at[m], q_r.at[m], mate(m))

    def q_half(m, h):
        at = pl.ds(h * half // 2, half // 2)
        k = 2 * (m - 1) + h
        return remote(q_send.at[at], q_in.at[m, at], q_s.at[k], q_r.at[k], mate(m))

    def q_relay(h):
        at = pl.ds(h * half // 2, half // 2)
        k = 4 + h
        return remote(
            q_in.at[1 + h, at], q_in.at[3, at], q_s.at[k], q_r.at[k], mate(2 - h)
        )

    def q_wait(m):
        if not relay:
            q_copy(m).wait_recv()
        elif m == 3:
            q_relay(0).wait_recv()
            q_relay(1).wait_recv()
        else:
            q_half(m, 2 - m).wait_recv()

    def p_copy(m):
        return remote(tab_send.at[m], tab_in.at[m], p_s.at[m], p_r.at[m], mate(m))

    def i_copy(m):
        return remote(pack, idx.at[m], i_s.at[m], i_r.at[m], mate(m))

    def o_copy(m):
        return remote(osend.at[m], orecv.at[m], o_s.at[m], o_r.at[m], mate(m))

    def t_copy(m):
        return remote(tsend.at[m], trecv.at[m], t_s.at[m], t_r.at[m], mate(m))

    def s_copy(m):
        return remote(ssend.at[m], srecv.at[chip], s_s.at[m], s_r.at[m], mate(m))

    with jax.named_scope("w_barrier"):
        pl.semaphore_wait(barrier, chips + z)
    for u in range(g - 1):

        @pl.when(u < z)
        def _():
            pl.semaphore_signal(up_sem, inc=1, device_id=(c, u), device_id_type=MESH)

    repeat(1, chips, lambda m: p_copy(m).start())
    if relay:
        for h in range(2):
            for m in (1, 2):
                q_half(m, (m - 1 + h) % 2).start()
    else:
        repeat(1, chips, lambda m: q_copy(chips - m).start())
    for t in range(PARTS):
        k_copy(t).start()
    e_copy().start()

    own_tab = pltpu.make_async_copy(tab_send.at[0], tabs.at[0], tab_sem.at[0])
    own_tab.start()

    early[2].wait()
    early[3].wait()
    for h in range(hb):
        piece = heads_ref[:, h * D_IDX : (h + 1) * D_IDX].astype(jnp.float32)
        for r in range(g):
            head_rows[r, h : h + 1, :] = piece[r : r + 1]
    eye = lax.broadcasted_iota(jnp.int32, (hb, hb), 0) == lax.broadcasted_iota(
        jnp.int32, (hb, hb), 1
    )
    gains = gains_ref[...].astype(jnp.float32)
    for r in range(g):
        mine_ref[r, 0] = head_rows[r].astype(jnp.bfloat16)
        gain = jnp.sum(jnp.where(eye, gains[r : r + 1], 0.0), axis=1, keepdims=True)
        mine_ref[r, 1] = jnp.broadcast_to(gain, (hb, D_IDX)).astype(jnp.bfloat16)

    own_z = pltpu.make_async_copy(mine_ref.at[z], zed.at[z], loc.at[0])
    own_z.start()
    for r in range(1, g):

        @pl.when(flip(z, r, g) < z)
        def _():
            z_copy(r).start()

    def turn_part(side, t):
        pages = part // PAGE
        kt[side, t * pages : (t + 1) * pages] = jnp.transpose(
            raw[side, :, t * part : (t + 1) * part]
        ).reshape(pages, PAGE, width)

    with jax.named_scope("xpose"):
        own_k.wait()
        for t in range(PARTS):
            turn_part(0, t)

    def rise():
        with jax.named_scope("w_up"):

            @pl.when(z < g - 1)
            def _():
                pl.semaphore_wait(up_sem, g - 1 - z)

        for r in range(1, g):

            @pl.when(flip(z, r, g) > z)
            def _():
                z_copy(r).start()

    def take_keys(t):
        k_copy(t).wait_recv()
        turn_part(1, t)

    def tab_copy(m):
        return pltpu.make_async_copy(tab_in.at[m], tabs.at[m], tab_sem.at[m])

    def take_tab(m):
        p_copy(m).wait_recv()
        tab_copy(m).start()

    for t in range(2):
        take_keys(t)
    pl.when(z > 0)(rise)

    with jax.named_scope("relay"):
        if relay:
            for h in range(2):
                q_half(1 + h, h).wait_recv()
                q_relay(h).start()

    pl.when(z == 0)(rise)

    with jax.named_scope("w_tab"):
        repeat(1, chips, take_tab)

    with jax.named_scope("w_k"):
        for t in range(2, PARTS):
            take_keys(t)

    with jax.named_scope("w_tab2"):
        own_tab.wait()
        repeat(1, chips, lambda m: tab_copy(m).wait())

    own_i = pltpu.make_async_copy(pack, idx.at[0], loc.at[3])

    def spread_index():
        with jax.named_scope("w_z"):
            own_z.wait()
            repeat(1, g, lambda r: z_copy(r).wait_recv())
            spread = lax.broadcasted_iota(jnp.int32, (hb, D_IDX), 1)
            blend = jnp.zeros((hb, D_IDX), jnp.float32)
            for r in range(g):
                pack[r] = zed[r, 0]
                blend = jnp.where(spread == r, zed[r, 1].astype(jnp.float32), blend)
            pack[g] = blend.astype(jnp.bfloat16)
            own_i.start()
            repeat(1, chips, lambda m: i_copy(m).start())

    scale = ((QK_NOPE + D_ROPE) ** -0.5) * LOG2E
    low = lax.broadcasted_iota(jnp.int32, (1, LANES), 1) < PAGE
    slots = 2 * most

    def attend(m):
        query = q_send[...] if isinstance(m, int) and m == 0 else q_in[m]
        queries[:half, :] = query[:, :width]
        queries[half:, :] = query[:, width:]
        ids = [tabs[m, 0, s] for s in range(slots)]
        flags = [jnp.minimum(p, 0).astype(jnp.float32) * -NEG for p in ids]
        keys = jnp.concatenate(
            [kt[s // most, jnp.maximum(ids[s], 0)] for s in range(slots)], axis=0
        )
        bias = jnp.concatenate(
            [jnp.where(low, flags[s], flags[s + 1]) for s in range(0, slots, 2)], axis=1
        )
        dots = lax.dot_general(
            queries[...], keys, (((1,), (1,)), ((), ())), preferred_element_type=jnp.float32
        ) * scale + bias
        top = jnp.max(dots, axis=1, keepdims=True)
        expo = jnp.exp2(dots - top)
        mass = jnp.sum(expo, axis=1, keepdims=True)
        mixed = jnp.dot(
            expo.astype(jnp.bfloat16), keys[:, :D_LAT], preferred_element_type=jnp.float32
        ).astype(jnp.bfloat16)
        osend[m, :, :D_LAT] = mixed[:half]
        osend[m, :, D_LAT:] = mixed[half:]
        lane = lax.broadcasted_iota(jnp.int32, (H, LANES), 1)
        tsend[m] = jnp.transpose(jnp.where(lane == 0, top, mass))[:8]

    def serve(m, between=None):
        with jax.named_scope("w_q"):
            q_wait(m)
        with jax.named_scope("att"):
            attend(m)
        if between is not None:
            between()
        t_copy(m).start()
        o_copy(m).start()

    count = g * hb
    block = min(256, ctx_dev)
    most_rows = min(4, chips)

    def lay(r):
        rows = idx[r]
        flat_query[r] = rows[:g].reshape(count, D_IDX)
        tile = rows[g].astype(jnp.float32)
        for u in range(g):
            wide_gains[r, u * hb : (u + 1) * hb] = jnp.broadcast_to(
                tile[:, u : u + 1], (hb, D_IDX)
            )

    def score(b):
        for s in range(2 * ctx_dev // block):
            at = (s * block) % ctx_dev
            keys = keys_all[s * block // ctx_dev, at : at + block, :]
            dots = lax.dot_general(
                flat_query[pl.ds(most_rows * b, most_rows)].reshape(most_rows * count, D_IDX),
                keys, (((1,), (1,)), ((), ())), preferred_element_type=jnp.float32,
            )
            for j in range(most_rows):
                gain = wide_gains[most_rows * b + j]
                for t in range(block // LANES):
                    total = jnp.sum(
                        jnp.maximum(
                            dots[j * count : (j + 1) * count, t * LANES : (t + 1) * LANES], 0.0
                        ) * gain,
                        axis=0, keepdims=True,
                    )
                    line = s * (block // LANES) + t
                    lines[most_rows * b + j, line : line + 1, :] = total

    def index_rows():
        with jax.named_scope("w_idx"):
            own_i.wait()
            own_e.wait()
            e_copy().wait_recv()
            repeat(1, chips, lambda m: i_copy(m).wait_recv())
        with jax.named_scope("index"):
            repeat(0, chips, lay)
            if chips > most_rows:

                def step(b, carry):
                    score(b)
                    return carry

                lax.fori_loop(0, chips // most_rows, step, 0)
            else:
                score(0)
            ssend[...] = lines[...].astype(jnp.bfloat16)
        repeat(1, chips, lambda m: s_copy(m).start())

    def own_rows():
        with jax.named_scope("att0"):
            attend(0)

    if chips <= 4:
        for m in range(1, chips):
            serve(m, spread_index if m == 1 else None)
        own_rows()
        index_rows()
    else:
        spread_index()
        repeat(1, chips, lambda m: serve(chips - m))
        index_rows()
        own_rows()
    own_s = pltpu.make_async_copy(ssend.at[0], srecv.at[chip], loc.at[4])
    own_s.start()

    def arrive(m):
        t_copy(m).wait_recv()
        o_copy(m).wait_recv()

    own_s.wait()

    def take_scores(m):
        remote(
            ssend.at[m], srecv.at[flip(chip, m, chips)], s_s.at[m], s_r.at[m], mate(m)
        ).wait_recv()

    with jax.named_scope("w_s"):
        repeat(1, chips, take_scores)
    with jax.named_scope("logp"):
        table = srecv[...].astype(jnp.float32)
        row_max = jnp.max(table)
        row_total = jnp.sum(jnp.exp(table - row_max), keepdims=True)
        logp_ref[...] = table - (row_max + jnp.log(row_total)) + jnp.log(
            jnp.full((1, 1, 1), n * ctx_dev, jnp.float32)
        )

    with jax.named_scope("w_o"):
        repeat(1, chips, arrive)
    with jax.named_scope("mix"):
        columns = [jnp.transpose(tsend[0] if m == 0 else trecv[m]) for m in range(chips)]
        tops = [v[:, 0:1] for v in columns]
        best = functools.reduce(jnp.maximum, tops)
        weights = [jnp.exp2(t - best) for t in tops]
        mass = functools.reduce(jnp.add, [w * v[:, 1:2] for w, v in zip(weights, columns)])
        shares = [w / mass for w in weights]
        for h in range(2):
            at = slice(h * D_LAT, (h + 1) * D_LAT)
            mixed = jnp.zeros((half, D_LAT), jnp.float32)
            for m in range(chips):
                value = osend[0, :, at] if m == 0 else orecv[m, :, at]
                mixed = mixed + value.astype(jnp.float32) * shares[m][h * half : (h + 1) * half]
            for p in range(half):
                start = (2 * p + h) * D_LAT
                out_ref[:, start : start + D_LAT] = mixed[p : p + 1].astype(jnp.bfloat16)

    with jax.named_scope("fin"):
        repeat(1, g, lambda r: z_copy(r).wait_send())
        for t in range(PARTS):
            k_copy(t).wait_send()
        e_copy().wait_send()

        def sent(m):
            p_copy(m).wait_send()
            if not relay:
                q_copy(m).wait_send()
            o_copy(m).wait_send()
            t_copy(m).wait_send()
            i_copy(m).wait_send()
            s_copy(m).wait_send()

        repeat(1, chips, sent)
        if relay:
            for h in range(2):
                q_half(1, h).wait_send()
                q_half(2, h).wait_send()
                q_relay(h).wait_send()


def per_device(n, g, idx_query, idx_weight, idx_keys, q_latent, latent_cache, page_ids):
    hb = H_IDX // g
    ctx_dev, width = idx_keys.shape[0], latent_cache.shape[1]
    chips = n // 2
    half = H // 2
    dma = pltpu.SemaphoreType.DMA
    bf16, f32, i32 = jnp.bfloat16, jnp.float32, jnp.int32
    hbm = pl.BlockSpec(memory_space=pltpu.HBM)
    vmem = pl.BlockSpec(memory_space=pltpu.VMEM)
    logp, out = pl.pallas_call(
        functools.partial(kernel, n, g),
        out_shape=(
            pltpu.VMEM((chips, 2 * ctx_dev // LANES, LANES), f32),
            pltpu.VMEM((1, H * D_LAT), bf16),
        ),
        in_specs=[hbm] * 6,
        out_specs=(vmem, vmem),
        scratch_shapes=[
            pltpu.VMEM(idx_query.shape, bf16),
            pltpu.VMEM(idx_weight.shape, bf16),
            pltpu.VMEM(q_latent.shape, bf16),
            pltpu.VMEM(page_ids.shape, i32),
            pltpu.VMEM((g, hb, D_IDX), f32),
            pltpu.VMEM((g, 2, hb, D_IDX), bf16),
            pltpu.VMEM((half, 2 * width), f32),
            pltpu.VMEM((half, 2 * width), bf16),
            pltpu.VMEM((chips, half, 2 * width), bf16),
            pltpu.VMEM((H, width), bf16),
            pltpu.VMEM((chips, g * hb, D_IDX), bf16),
            pltpu.VMEM((chips, g * hb, D_IDX), f32),
            pltpu.VMEM((g, 2, hb, D_IDX), bf16),
            pltpu.VMEM((g + 1, hb, D_IDX), bf16),
            pltpu.VMEM((chips, g + 1, hb, D_IDX), bf16),
            pltpu.VMEM((2, ctx_dev, D_IDX), bf16),
            pltpu.VMEM((2, width, ctx_dev), bf16),
            pltpu.VMEM((2, ctx_dev // PAGE, PAGE, width), bf16),
            pltpu.VMEM((chips, 1, LANES), i32),
            pltpu.VMEM((chips, 1, LANES), i32),
            pltpu.SMEM((chips, 1, LANES), i32),
            pltpu.VMEM((chips, 2 * ctx_dev // LANES, LANES), f32),
            pltpu.VMEM((chips, half, 2 * D_LAT), bf16),
            pltpu.VMEM((chips, half, 2 * D_LAT), bf16),
            pltpu.VMEM((chips, 8, LANES), f32),
            pltpu.VMEM((chips, 8, LANES), f32),
            pltpu.VMEM((chips, 2 * ctx_dev // LANES, LANES), bf16),
            pltpu.VMEM((chips, 2 * ctx_dev // LANES, LANES), bf16),
            pltpu.SemaphoreType.REGULAR,
            dma((g,)), dma((g,)),
            dma((chips,)), dma((chips,)),
            dma((PARTS,)), dma((PARTS,)),
            dma((max(6, chips),)), dma((max(6, chips),)),
            dma((chips,)), dma((chips,)),
            dma((chips,)), dma((chips,)),
            dma((chips,)), dma((chips,)),
            dma((chips,)), dma((chips,)),
            dma, dma,
            dma((10,)), dma((chips,)),
        ],
        compiler_params=pltpu.CompilerParams(
            collective_id=0, has_side_effects=True, vmem_limit_bytes=VMEM_MIB * 1024 * 1024
        ),
    )(idx_query, idx_weight, latent_cache.T, idx_keys, q_latent, page_ids)
    return logp.reshape(1, n * ctx_dev), out


def solution(mesh):
    in_specs = (
        P("ctx", "qry"),
        P("ctx", "qry"),
        P("ctx", None),
        P(("ctx", "qry"), None),
        P("ctx", None),
        P(("ctx", "qry"), None),
    )
    out_specs = (P(("ctx", "qry"), None), P(("ctx", "qry"), None))
    return jax.shard_map(
        functools.partial(per_device, mesh.shape["ctx"], mesh.shape["qry"]),
        mesh=mesh, in_specs=in_specs, out_specs=out_specs, check_vma=False,
    )
```
